32 devices in a mesh: chan: 16 (over z, x, core), tm: 2 (over y).
Axes of the slice: x: 2, y: 2, z: 4, core: 2. Of those that a mesh axis runs over, the one named last changes fastest.
Arguments:
- samples: bfloat16 [2, 256, 32, 1024], P(None, 'chan', 'tm'), may hold values from -64 to 64
- steer_index: int32 [256, 256], replicated, may hold values from 0 to 255
Outputs:
- beams: bfloat16 [2, 128, 256, 32], P(None, 'chan', None, 'tm')
The draws below stay inside these ranges and needn't reach their ends.
All inputs are finite; a program needn't handle non-finite values.
Results may differ from the reference program's by a relative error of at most 0.0081.
Values may be sent and summed in bfloat16 or wider, within the bound.
A program may use at most 128 MiB of HBM per device.

```python
import math
import jax
import jax.numpy as jnp
from jax import lax

A = 256
C = 1024
B = 256
PHASES = 256
ITERS = 3
BAND = 128
SNAPS = 32


def draw_samples(key, part):
    keys = jax.random.split(key, 4)
    sources = 8
    phase_angle = jax.random.uniform(keys[0], (sources, A), jnp.float32, -math.pi, math.pi)
    strength = jnp.exp(jax.random.uniform(keys[1], (sources,), jnp.float32, math.log(0.3), math.log(1.0)))
    noise_scale = jnp.exp(jax.random.uniform(keys[2], (A,), jnp.float32, math.log(0.5), math.log(2.0)))
    signal = jax.random.normal(keys[3], (2, sources, SNAPS * C), jnp.float32)
    mix_real = strength[:, None] * jnp.cos(phase_angle)
    mix_imag = strength[:, None] * jnp.sin(phase_angle)

    def one_antenna(antenna):
        noise_key = jax.random.fold_in(key, antenna + 17)
        column_real = mix_real[:, antenna]
        column_imag = mix_imag[:, antenna]
        real_part = jnp.dot(column_real, signal[0]) - jnp.dot(column_imag, signal[1])
        imag_part = jnp.dot(column_real, signal[1]) + jnp.dot(column_imag, signal[0])
        noise = jax.random.normal(noise_key, (2, SNAPS * C), jnp.float32)
        mixed = jnp.stack([real_part, imag_part], 0) + noise_scale[antenna] * noise
        return jnp.clip(mixed, -64.0, 64.0).astype(jnp.bfloat16)
    drawn = lax.map(one_antenna, jnp.arange(A, dtype=jnp.int32))
    return jnp.transpose(drawn, (1, 0, 2)).reshape(2, A, SNAPS, C)


def set_ends(values, stream_key, low, high):
    dims = values.shape
    place = [jax.random.randint(jax.random.fold_in(stream_key, axis), (), 0, dims[axis]) for axis in range(len(dims))]
    values = values.at[tuple(place)].set(low)
    longest = dims.index(max(dims))
    place[longest] = (place[longest] + 1) % dims[longest]
    return values.at[tuple(place)].set(high)


def setup_inputs(seed: int = 0) -> dict:
    splits = jax.random.split(jax.random.key(seed), 3)
    return {
        "samples": draw_samples(jax.random.fold_in(splits[2], 71), 0),
        "steer_index": set_ends(jax.random.randint(splits[1], (B, A), 0, PHASES), jax.random.fold_in(splits[1], 1), 0, PHASES - 1).astype(jnp.int32),
    }


HIGHEST = lax.Precision.HIGHEST

def transform_table(channels_all):
    offset = (C - channels_all) // 2
    channel_number = jnp.arange(channels_all, dtype=jnp.int32) + offset
    sample_number = jnp.arange(C, dtype=jnp.int32)
    phase_turns = channel_number[:, None] * sample_number[None, :] % C
    phase_angle = 2.0 * math.pi / C * phase_turns.astype(jnp.float32)
    window_taper = (0.5 - 0.5 * jnp.cos(2.0 * math.pi / C * sample_number.astype(jnp.float32))) / math.sqrt(C)
    cosine = window_taper[None, :] * jnp.cos(phase_angle)
    sine_part = window_taper[None, :] * jnp.sin(phase_angle)
    coefficients = jnp.stack([jnp.stack([cosine, sine_part], 1), jnp.stack([-sine_part, cosine], 1)], 0)
    return coefficients.astype(jnp.bfloat16)

def complex_product(left_real, left_imag, right_real, right_imag):
    real_part = jnp.dot(left_real, right_real, precision=HIGHEST) - jnp.dot(left_imag, right_imag, precision=HIGHEST)
    imag_part = jnp.dot(left_real, right_imag, precision=HIGHEST) + jnp.dot(left_imag, right_real, precision=HIGHEST)
    return (real_part, imag_part)

def invert_loaded(covariance_real, covariance_imag):
    matrix_order = covariance_real.shape[0]
    loading = 0.1 * jnp.mean(jnp.diagonal(covariance_real))
    identity = jnp.eye(matrix_order, dtype=jnp.float32)
    loaded = covariance_real + loading * identity
    magnitude = jnp.sqrt(loaded * loaded + covariance_imag * covariance_imag)
    largest = jnp.max(lax.optimization_barrier(jnp.sum(magnitude, axis=1)))

    def iterate(counter, state):
        approx_real, approx_imag = state
        image_real, image_imag = complex_product(loaded, covariance_imag, approx_real, approx_imag)
        square_real, square_imag = complex_product(approx_real, approx_imag, image_real, image_imag)
        return (2.0 * approx_real - square_real, 2.0 * approx_imag - square_imag)
    start_state = (identity / largest, jnp.zeros_like(identity))
    return lax.fori_loop(0, ITERS, iterate, start_state)

def form_weights(covariance_real, covariance_imag, steer_real, steer_imag):
    inverse_real, inverse_imag = invert_loaded(covariance_real, covariance_imag)
    gain_real, gain_imag = complex_product(inverse_real, inverse_imag, steer_real, steer_imag)
    response = lax.optimization_barrier(jnp.sum(steer_real * gain_real + steer_imag * gain_imag, axis=0))
    factor = lax.rsqrt(response)
    return ((gain_real * factor).astype(jnp.bfloat16), (gain_imag * factor).astype(jnp.bfloat16))

def steering(steer_index):
    phase_angle = 2.0 * math.pi / PHASES * steer_index.astype(jnp.float32)
    return (jnp.cos(phase_angle).T, jnp.sin(phase_angle).T)

def channel_beams(spectrum, steer_real, steer_imag):
    values = spectrum.astype(jnp.float32)
    outer_sums = jnp.einsum('ins,jms->injm', values, values, precision=HIGHEST)
    covariance_real = (outer_sums[0, :, 0, :] + outer_sums[1, :, 1, :]) / SNAPS
    covariance_imag = (outer_sums[1, :, 0, :] - outer_sums[0, :, 1, :]) / SNAPS
    weight_real, weight_imag = form_weights(covariance_real, covariance_imag, steer_real, steer_imag)
    real_weight = weight_real.astype(jnp.float32)
    imag_weight = weight_imag.astype(jnp.float32)
    beam_real = jnp.einsum('nb,ns->bs', real_weight, values[0], precision=HIGHEST) + jnp.einsum('nb,ns->bs', imag_weight, values[1], precision=HIGHEST)
    beam_imag = jnp.einsum('nb,ns->bs', real_weight, values[1], precision=HIGHEST) - jnp.einsum('nb,ns->bs', imag_weight, values[0], precision=HIGHEST)
    return jnp.stack([beam_real, beam_imag], 0).astype(jnp.bfloat16)

def reference(samples, steer_index):
    coefficients = transform_table(BAND).astype(jnp.float32)

    def antenna_spectra(antenna_samples):
        spectrum = lax.dot_general(coefficients, antenna_samples.astype(jnp.float32), (((2, 3), (0, 2)), ((), ())), precision=HIGHEST)
        return spectrum.astype(jnp.bfloat16)
    per_antenna = lax.map(antenna_spectra, jnp.transpose(samples, (1, 0, 2, 3)))
    by_channel = jnp.transpose(per_antenna, (2, 1, 0, 3))
    steer_real, steer_imag = steering(steer_index)
    beams = lax.map(lambda spectrum: channel_beams(spectrum, steer_real, steer_imag), by_channel)
    return jnp.transpose(beams, (1, 0, 2, 3))
```

```python
import functools
import math

import jax
import jax.numpy as jnp
import numpy as np
from jax import lax
from jax.experimental import pallas as pl
from jax.experimental.pallas import tpu as pltpu
from jax.sharding import PartitionSpec as P

C = 1024
PHASES = 256
CH_DEV = 8
ITERS = 3
TERMS = 2**ITERS
LANES = 128


HIGHEST = lax.Precision.HIGHEST
F32 = jnp.float32
BF16 = jnp.bfloat16
NT = (((1,), (1,)), ((), ()))


def transform_table(channels_all):
    offset = (C - channels_all) // 2
    channel_number = jnp.arange(channels_all, dtype=jnp.int32) + offset
    sample_number = jnp.arange(C, dtype=jnp.int32)
    phase_turns = channel_number[:, None] * sample_number[None, :] % C
    phase_angle = 2.0 * math.pi / C * phase_turns.astype(jnp.float32)
    window_taper = (
        0.5 - 0.5 * jnp.cos(2.0 * math.pi / C * sample_number.astype(jnp.float32))
    ) / math.sqrt(C)
    cosine = window_taper[None, :] * jnp.cos(phase_angle)
    sine_part = window_taper[None, :] * jnp.sin(phase_angle)
    coefficients = jnp.stack(
        [jnp.stack([cosine, sine_part], 1), jnp.stack([-sine_part, cosine], 1)], 0
    )
    return coefficients.astype(jnp.bfloat16)


def complex_product(left_real, left_imag, right_real, right_imag):
    real_part = jnp.dot(left_real, right_real, precision=HIGHEST) - jnp.dot(
        left_imag, right_imag, precision=HIGHEST
    )
    imag_part = jnp.dot(left_real, right_imag, precision=HIGHEST) + jnp.dot(
        left_imag, right_real, precision=HIGHEST
    )
    return (real_part, imag_part)


def invert_loaded(covariance_real, covariance_imag):
    matrix_order = covariance_real.shape[0]
    loading = 0.1 * jnp.mean(jnp.diagonal(covariance_real))
    identity = jnp.eye(matrix_order, dtype=jnp.float32)
    loaded = covariance_real + loading * identity
    magnitude = jnp.sqrt(loaded * loaded + covariance_imag * covariance_imag)
    largest = jnp.max(jnp.sum(magnitude, axis=1))

    def iterate(counter, state):
        approx_real, approx_imag = state
        image_real, image_imag = complex_product(loaded, covariance_imag, approx_real, approx_imag)
        square_real, square_imag = complex_product(approx_real, approx_imag, image_real, image_imag)
        return (2.0 * approx_real - square_real, 2.0 * approx_imag - square_imag)

    start_state = (identity / largest, jnp.zeros_like(identity))
    return lax.fori_loop(0, ITERS, iterate, start_state)


def form_weights(covariance_real, covariance_imag, steer_real, steer_imag):
    inverse_real, inverse_imag = invert_loaded(covariance_real, covariance_imag)
    gain_real, gain_imag = complex_product(inverse_real, inverse_imag, steer_real, steer_imag)
    response = jnp.sum(steer_real * gain_real + steer_imag * gain_imag, axis=0)
    factor = lax.rsqrt(response)
    return ((gain_real * factor).astype(jnp.bfloat16), (gain_imag * factor).astype(jnp.bfloat16))


def weights_stacked(covariance_real, covariance_imag, steer_real, steer_imag):
    weight_real, weight_imag = jax.vmap(form_weights, in_axes=(0, 0, None, None))(
        covariance_real, covariance_imag, steer_real, steer_imag
    )
    return jnp.stack([weight_real, weight_imag], 1)


def steering(steer_index):
    phase_angle = 2.0 * math.pi / PHASES * steer_index.astype(jnp.float32)
    return (jnp.cos(phase_angle).T, jnp.sin(phase_angle).T)


def apply_beams(weight_pair, spectrum):
    real_weight = weight_pair[:, 0]
    imag_weight = weight_pair[:, 1]
    beam_real = jnp.einsum(
        "knb,kns->kbs", real_weight, spectrum[0], preferred_element_type=jnp.float32
    ) + jnp.einsum("knb,kns->kbs", imag_weight, spectrum[1], preferred_element_type=jnp.float32)
    beam_imag = jnp.einsum(
        "knb,kns->kbs", real_weight, spectrum[1], preferred_element_type=jnp.float32
    ) - jnp.einsum("knb,kns->kbs", imag_weight, spectrum[0], preferred_element_type=jnp.float32)
    return jnp.stack([beam_real, beam_imag], 0).astype(jnp.bfloat16)


def local(samples, steer_index):
    channels_all = CH_DEV * lax.axis_size("chan")
    coefficients = transform_table(channels_all)
    spectra = lax.dot_general(
        coefficients, samples, (((2, 3), (0, 3)), ((), ())), preferred_element_type=jnp.float32
    ).astype(jnp.bfloat16)
    steer_real, steer_imag = steering(steer_index)
    turned = lax.all_to_all(
        lax.all_to_all(spectra, "chan", split_axis=1, concat_axis=2, tiled=True),
        "tm",
        split_axis=1,
        concat_axis=3,
        tiled=True,
    )
    outer_sums = jnp.einsum("ikns,jkms->kinjm", turned, turned, preferred_element_type=jnp.float32)
    snapshots = turned.shape[3]
    covariance_real = (outer_sums[:, 0, :, 0, :] + outer_sums[:, 1, :, 1, :]) / snapshots
    covariance_imag = (outer_sums[:, 1, :, 0, :] - outer_sums[:, 0, :, 1, :]) / snapshots
    weight_pair = weights_stacked(covariance_real, covariance_imag, steer_real, steer_imag)
    local_beams = apply_beams(weight_pair, turned)
    return lax.all_to_all(local_beams, "tm", split_axis=3, concat_axis=1, tiled=True)


def taper_table(channels_all):
    offset = (C - channels_all) // 2
    channel = np.arange(channels_all) + offset
    sample = np.arange(C)
    angle = 2.0 * math.pi / C * (channel[None, :] * sample[:, None] % C)
    taper = (0.5 - 0.5 * np.cos(2.0 * math.pi / C * sample)) / math.sqrt(C)
    both = np.concatenate([taper[:, None] * np.cos(angle), taper[:, None] * np.sin(angle)], 1)
    return both.astype(np.float32).astype(BF16)


def iota(shape, axis):
    return lax.broadcasted_iota(jnp.int32, shape, axis)


def dot(a, b, dims=(((1,), (0,)), ((), ()))):
    return lax.dot_general(a, b, dims, preferred_element_type=F32)


def split(x):
    high = x.astype(BF16)
    return high, (x - high.astype(F32)).astype(BF16)


def dot3(a, b):
    (ah, al), (bh, bl) = a, b
    return dot(ah, bh) + (dot(ah, bl) + dot(al, bh))


def exchange_blocks(rows, count, width):
    lane = iota(rows[0].shape, 1)
    total = count * width
    step = count // 2
    while step:
        low = (lane // width) & step == 0
        done = list(rows)
        for a in range(count):
            if a & step:
                continue
            b = a + step
            up = pltpu.roll(rows[b], step * width, 1)
            down = pltpu.roll(rows[a], total - step * width, 1)
            done[a] = jnp.where(low, rows[a], up)
            done[b] = jnp.where(low, down, rows[b])
        rows = done
        step //= 2
    return rows


def steering_parts(index):
    turn = index & (PHASES - 1)
    quarter = PHASES // 4
    quadrant = (turn + quarter // 2) // quarter
    x = (turn - quarter * quadrant).astype(F32) * (2.0 * math.pi / PHASES)
    y = x * x
    s = x * (1.0 + y * (-1.0 / 6 + y * (1.0 / 120 + y * (-1.0 / 5040 + y * (1.0 / 362880)))))
    c = 1.0 + y * (-0.5 + y * (1.0 / 24 + y * (-1.0 / 720 + y * (1.0 / 40320 - y * (1.0 / 3628800)))))
    odd = quadrant & 1 == 1
    flip_c = (quadrant + 1) & 2 == 2
    flip_s = quadrant & 2 == 2
    cosine = jnp.where(odd, s, c)
    sine = jnp.where(odd, c, s)
    return jnp.where(flip_c, -cosine, cosine), jnp.where(flip_s, -sine, sine)


def fused(ni, nj, samples_ref, table_ref, index_ref, out_ref, re_ref, im_ref, send_ref, recv_ref,
          steer_ref, x_ref, p_ref, send_sem, recv_sem):
    nl, t_loc, q = 16, 16, 2 * CH_DEV
    antennas = ni * nl
    size = q * t_loc
    devices = ni * nj
    my_i, my_j = lax.axis_index("chan"), lax.axis_index("tm")
    me = my_i * nj + my_j

    barrier = pltpu.get_barrier_semaphore()

    def greet(step, carry):
        peer = lax.rem(me + step, devices)
        pl.semaphore_signal(barrier, inc=1, device_id=(peer // nj, lax.rem(peer, nj)),
                            device_id_type=pl.DeviceIdType.MESH)
        return carry

    lax.fori_loop(1, devices, greet, 0)

    table = table_ref[...]
    half = table.shape[1] // 2
    first = dot(samples_ref[0], table)
    second = dot(samples_ref[1], table)
    re_ref[...] = first[:, :half] + second[:, half:]
    im_ref[...] = second[:, :half] - first[:, half:]
    parts = []
    for ref in (re_ref, im_ref):
        rows = [ref[pl.ds(t, nl, stride=t_loc), :] for t in range(t_loc)]
        parts.append(exchange_blocks(rows, ni, CH_DEV))
    blocks = jnp.concatenate(
        [jnp.concatenate([a, b], 1) for a, b in zip(*parts)], 0
    ).astype(BF16)
    src, dst = iota((size, size), 0), iota((size, size), 1)
    want = (dst // t_loc % 2) * (t_loc * CH_DEV) + (dst % t_loc) * CH_DEV + dst // (2 * t_loc)
    order = jnp.where(src == want, 1.0, 0.0).astype(BF16)
    send_ref[...] = dot(blocks, order).astype(BF16)

    pl.semaphore_wait(barrier, devices - 1)

    def copy_to(peer, slot):
        to_i, to_j = peer // nj, lax.rem(peer, nj)
        return pltpu.make_async_remote_copy(
            src_ref=send_ref.at[pl.ds(pl.multiple_of(to_i * nl, nl), nl), :],
            dst_ref=recv_ref.at[my_j, pl.ds(pl.multiple_of(my_i * nl, nl), nl), :],
            send_sem=send_sem.at[slot],
            recv_sem=recv_sem.at[me],
            device_id=(to_i, to_j),
            device_id_type=pl.DeviceIdType.MESH,
        )

    def send(step, carry):
        copy_to(lax.rem(me + step, devices), step).start()
        return carry

    lax.fori_loop(1, devices, send, 0)
    mine = pl.ds(pl.multiple_of(my_i * nl, nl), nl)
    recv_ref[my_j, mine, :] = send_ref[mine, :]

    cosine, sine = steering_parts(index_ref[...])
    steer_ref[0], steer_ref[1] = split(cosine)
    steer_ref[2], steer_ref[3] = split(sine)

    def arrive(step, carry):
        peer = lax.rem(me + step, devices)
        from_i, from_j = peer // nj, lax.rem(peer, nj)
        pltpu.make_async_remote_copy(
            src_ref=send_ref.at[mine, :],
            dst_ref=recv_ref.at[from_j, pl.ds(pl.multiple_of(from_i * nl, nl), nl), :],
            send_sem=send_sem.at[step],
            recv_sem=recv_sem.at[peer],
            device_id=(from_i, from_j),
            device_id_type=pl.DeviceIdType.MESH,
        ).wait_recv()
        return carry

    lax.fori_loop(1, devices, arrive, 0)

    groups = size // LANES
    per = CH_DEV // groups
    cols = nj * LANES
    row_id, col_id = iota((cols, cols), 0), iota((cols, cols), 1)
    chan_of = lambda x: x // (2 * t_loc) % per
    same = chan_of(row_id) == chan_of(col_id)
    on_diag = row_id == col_id
    unit = jnp.where(on_diag, 1.0, 0.0).astype(BF16)
    turn_j = jnp.where(row_id == (col_id ^ t_loc), jnp.where(col_id & t_loc == 0, 1.0, -1.0), 0.0).astype(BF16)
    lane_chan = chan_of(iota((1, cols), 1))
    span = 2 * t_loc
    tiles = range(cols // span)

    def by_channel(values):
        return jnp.concatenate([jnp.broadcast_to(values[i % per], (span, cols)) for i in tiles], 0)

    for g in range(groups):
        z = jnp.concatenate([recv_ref[j, :, g * LANES : (g + 1) * LANES] for j in range(nj)], 1)
        zt = dot(unit, z, NT).astype(BF16)
        zj = dot(z, turn_j).astype(BF16)
        zjt = jnp.concatenate(
            [b for i in range(cols // span) for b in
             (zt[i * span + t_loc : (i + 1) * span], -zt[i * span : i * span + t_loc])], 0)
        gram = dot(zt, z) + dot(zjt, zj)
        pt = (dot(zt, steer_ref[0], NT) + dot(zt, steer_ref[1], NT)) + (
            dot(zjt, steer_ref[2], NT) + dot(zjt, steer_ref[3], NT))
        diagonal = jnp.where(on_diag, gram, 0.0)
        bounds, rhos = [], []
        for k in range(per):
            keep = jnp.where(lane_chan == k, 1.0, 0.0).astype(BF16)
            cov_re = dot(z * keep, zt)
            cov_im = dot(zj * keep, zt)
            power = cov_re * cov_re + cov_im * cov_im
            magnitude = power * lax.rsqrt(jnp.maximum(power, 1e-37))
            largest = jnp.max(jnp.sum(magnitude, axis=0, keepdims=True), axis=1, keepdims=True)
            trace = 0.0
            for j in range(nj):
                at = j * LANES + k * span
                trace += jnp.sum(jnp.sum(diagonal[at : at + span], axis=0, keepdims=True), axis=1, keepdims=True)
            load = (0.1 / antennas * 0.5) * trace
            bound = largest + load
            bounds.append(bound)
            rhos.append(1.0 - load / bound)
        sums = []
        for k in range(per):
            s, total = [], 1.0 + 0.0 * rhos[k]
            for m in range(TERMS):
                s.append(total)
                total = 1.0 + rhos[k] * total
            sums.append(s)
        inverse = [1.0 / b for b in bounds]
        x = jnp.where(same, gram, 0.0) * by_channel(inverse)
        r1 = jnp.where(on_diag, by_channel(rhos), 0.0) - x
        s1 = split(r1)
        r2 = dot3(s1, s1)
        s2 = split(r2)
        r3 = dot3(s2, s1)
        coef = lambda i: by_channel([sums[k][TERMS - 2 - i] for k in range(per)])
        tail = jnp.where(on_diag, coef(3), 0.0) + coef(4) * r1 + coef(5) * r2 + coef(6) * r3
        poly = (jnp.where(on_diag, coef(0), 0.0) + coef(1) * r1 + coef(2) * r2) + dot3(split(r3), split(tail))
        vt = dot3(split(poly), split(pt))
        product = pt * vt
        x_ref[...] = x
        p_ref[...] = pt
        own = pl.ds(pl.multiple_of(my_j * LANES, LANES), LANES)
        back = dot3(split(x_ref[own, :]), split(vt))
        mine_p = p_ref[own, :]
        for k in range(per):
            at = k * span
            energy = 0.0
            for j in range(nj):
                low = j * LANES + at
                energy += jnp.sum(product[low : low + span], axis=0, keepdims=True)
            whole = sums[k][TERMS - 1]
            response = antennas * whole - energy * inverse[k]
            factor = lax.rsqrt(response) * lax.rsqrt(bounds[k] * (1.0 / (nj * t_loc)))
            beam = (whole * mine_p[at : at + span] - back[at : at + span]) * factor
            beam = beam.astype(BF16)
            out_ref[0, g * per + k] = beam[:t_loc]
            out_ref[1, g * per + k] = beam[t_loc:]

    def drain(step, carry):
        copy_to(lax.rem(me + step, devices), step).wait_send()
        return carry

    lax.fori_loop(1, devices, drain, 0)


def fused_local(ni, nj, samples, steer_index):
    _, nl, t_loc, _ = samples.shape
    beams, antennas = steer_index.shape
    size = 2 * CH_DEV * t_loc
    cols = nj * LANES
    vmem = pl.BlockSpec(memory_space=pltpu.VMEM)
    table = jnp.asarray(taper_table(CH_DEV * ni))
    out = pl.pallas_call(
        functools.partial(fused, ni, nj),
        out_shape=jax.ShapeDtypeStruct((2, CH_DEV, t_loc, beams), BF16),
        in_specs=[vmem] * 3,
        out_specs=vmem,
        scratch_shapes=[
            pltpu.VMEM((nl * t_loc, CH_DEV * ni), F32),
            pltpu.VMEM((nl * t_loc, CH_DEV * ni), F32),
            pltpu.VMEM((antennas, size), BF16),
            pltpu.VMEM((nj, antennas, size), BF16),
            pltpu.VMEM((4, beams, antennas), BF16),
            pltpu.VMEM((cols, cols), F32),
            pltpu.VMEM((cols, beams), F32),
            pltpu.SemaphoreType.DMA((ni * nj,)),
            pltpu.SemaphoreType.DMA((ni * nj,)),
        ],
        compiler_params=pltpu.CompilerParams(collective_id=0, has_side_effects=True),
    )(samples.reshape(2, nl * t_loc, C), table, steer_index)
    return jnp.transpose(out, (0, 1, 3, 2))


def choose(ni, nj, samples, steer_index):
    _, nl, t_loc, _ = samples.shape
    beams, antennas = steer_index.shape
    tiled = nl == 16 and t_loc == 16 and CH_DEV * ni == LANES and antennas == nl * ni
    if tiled and nj * LANES == antennas:
        return fused_local(ni, nj, samples, steer_index)
    return local(samples, steer_index)


def solution(mesh):
    return jax.shard_map(
        functools.partial(choose, mesh.shape["chan"], mesh.shape["tm"]),
        mesh=mesh,
        in_specs=(P(None, "chan", "tm", None), P()),
        out_specs=P(None, "chan", None, "tm"),
        check_vma=False,
    )
```

```python
import functools
import math

import jax
import jax.numpy as jnp
import numpy as np
from jax import lax
from jax.experimental import pallas as pl
from jax.experimental.pallas import tpu as pltpu
from jax.sharding import PartitionSpec as P

C = 1024
PHASES = 256
CH_DEV = 8
ITERS = 3
TERMS = 2**ITERS
LANES = 128


HIGHEST = lax.Precision.HIGHEST
F32 = jnp.float32
BF16 = jnp.bfloat16
NT = (((1,), (1,)), ((), ()))


def transform_table(channels_all):
    offset = (C - channels_all) // 2
    channel_number = jnp.arange(channels_all, dtype=jnp.int32) + offset
    sample_number = jnp.arange(C, dtype=jnp.int32)
    phase_turns = channel_number[:, None] * sample_number[None, :] % C
    phase_angle = 2.0 * math.pi / C * phase_turns.astype(jnp.float32)
    window_taper = (
        0.5 - 0.5 * jnp.cos(2.0 * math.pi / C * sample_number.astype(jnp.float32))
    ) / math.sqrt(C)
    cosine = window_taper[None, :] * jnp.cos(phase_angle)
    sine_part = window_taper[None, :] * jnp.sin(phase_angle)
    coefficients = jnp.stack(
        [jnp.stack([cosine, sine_part], 1), jnp.stack([-sine_part, cosine], 1)], 0
    )
    return coefficients.astype(jnp.bfloat16)


def complex_product(left_real, left_imag, right_real, right_imag):
    real_part = jnp.dot(left_real, right_real, precision=HIGHEST) - jnp.dot(
        left_imag, right_imag, precision=HIGHEST
    )
    imag_part = jnp.dot(left_real, right_imag, precision=HIGHEST) + jnp.dot(
        left_imag, right_real, precision=HIGHEST
    )
    return (real_part, imag_part)


def invert_loaded(covariance_real, covariance_imag):
    matrix_order = covariance_real.shape[0]
    loading = 0.1 * jnp.mean(jnp.diagonal(covariance_real))
    identity = jnp.eye(matrix_order, dtype=jnp.float32)
    loaded = covariance_real + loading * identity
    magnitude = jnp.sqrt(loaded * loaded + covariance_imag * covariance_imag)
    largest = jnp.max(jnp.sum(magnitude, axis=1))

    def iterate(counter, state):
        approx_real, approx_imag = state
        image_real, image_imag = complex_product(loaded, covariance_imag, approx_real, approx_imag)
        square_real, square_imag = complex_product(approx_real, approx_imag, image_real, image_imag)
        return (2.0 * approx_real - square_real, 2.0 * approx_imag - square_imag)

    start_state = (identity / largest, jnp.zeros_like(identity))
    return lax.fori_loop(0, ITERS, iterate, start_state)


def form_weights(covariance_real, covariance_imag, steer_real, steer_imag):
    inverse_real, inverse_imag = invert_loaded(covariance_real, covariance_imag)
    gain_real, gain_imag = complex_product(inverse_real, inverse_imag, steer_real, steer_imag)
    response = jnp.sum(steer_real * gain_real + steer_imag * gain_imag, axis=0)
    factor = lax.rsqrt(response)
    return ((gain_real * factor).astype(jnp.bfloat16), (gain_imag * factor).astype(jnp.bfloat16))


def weights_stacked(covariance_real, covariance_imag, steer_real, steer_imag):
    weight_real, weight_imag = jax.vmap(form_weights, in_axes=(0, 0, None, None))(
        covariance_real, covariance_imag, steer_real, steer_imag
    )
    return jnp.stack([weight_real, weight_imag], 1)


def steering(steer_index):
    phase_angle = 2.0 * math.pi / PHASES * steer_index.astype(jnp.float32)
    return (jnp.cos(phase_angle).T, jnp.sin(phase_angle).T)


def apply_beams(weight_pair, spectrum):
    real_weight = weight_pair[:, 0]
    imag_weight = weight_pair[:, 1]
    beam_real = jnp.einsum(
        "knb,kns->kbs", real_weight, spectrum[0], preferred_element_type=jnp.float32
    ) + jnp.einsum("knb,kns->kbs", imag_weight, spectrum[1], preferred_element_type=jnp.float32)
    beam_imag = jnp.einsum(
        "knb,kns->kbs", real_weight, spectrum[1], preferred_element_type=jnp.float32
    ) - jnp.einsum("knb,kns->kbs", imag_weight, spectrum[0], preferred_element_type=jnp.float32)
    return jnp.stack([beam_real, beam_imag], 0).astype(jnp.bfloat16)


def local(samples, steer_index):
    channels_all = CH_DEV * lax.axis_size("chan")
    coefficients = transform_table(channels_all)
    spectra = lax.dot_general(
        coefficients, samples, (((2, 3), (0, 3)), ((), ())), preferred_element_type=jnp.float32
    ).astype(jnp.bfloat16)
    steer_real, steer_imag = steering(steer_index)
    turned = lax.all_to_all(
        lax.all_to_all(spectra, "chan", split_axis=1, concat_axis=2, tiled=True),
        "tm",
        split_axis=1,
        concat_axis=3,
        tiled=True,
    )
    outer_sums = jnp.einsum("ikns,jkms->kinjm", turned, turned, preferred_element_type=jnp.float32)
    snapshots = turned.shape[3]
    covariance_real = (outer_sums[:, 0, :, 0, :] + outer_sums[:, 1, :, 1, :]) / snapshots
    covariance_imag = (outer_sums[:, 1, :, 0, :] - outer_sums[:, 0, :, 1, :]) / snapshots
    weight_pair = weights_stacked(covariance_real, covariance_imag, steer_real, steer_imag)
    local_beams = apply_beams(weight_pair, turned)
    return lax.all_to_all(local_beams, "tm", split_axis=3, concat_axis=1, tiled=True)


def taper_table(channels_all):
    offset = (C - channels_all) // 2
    channel = np.arange(channels_all) + offset
    sample = np.arange(C)
    angle = 2.0 * math.pi / C * (channel[None, :] * sample[:, None] % C)
    taper = (0.5 - 0.5 * np.cos(2.0 * math.pi / C * sample)) / math.sqrt(C)
    both = np.concatenate([taper[:, None] * np.cos(angle), taper[:, None] * np.sin(angle)], 1)
    return both.astype(np.float32).astype(BF16)


def iota(shape, axis):
    return lax.broadcasted_iota(jnp.int32, shape, axis)


def dot(a, b, dims=(((1,), (0,)), ((), ()))):
    return lax.dot_general(a, b, dims, preferred_element_type=F32)


def split(x):
    high = x.astype(BF16)
    return high, (x - high.astype(F32)).astype(BF16)


def dot3(a, b):
    (ah, al), (bh, bl) = a, b
    return dot(ah, bh) + (dot(ah, bl) + dot(al, bh))


def exchange_blocks(rows, count, width):
    lane = iota(rows[0].shape, 1)
    total = count * width
    step = count // 2
    while step:
        low = (lane // width) & step == 0
        done = list(rows)
        for a in range(count):
            if a & step:
                continue
            b = a + step
            up = pltpu.roll(rows[b], step * width, 1)
            down = pltpu.roll(rows[a], total - step * width, 1)
            done[a] = jnp.where(low, rows[a], up)
            done[b] = jnp.where(low, down, rows[b])
        rows = done
        step //= 2
    return rows


def steering_parts(index):
    turn = index & (PHASES - 1)
    quarter = PHASES // 4
    quadrant = (turn + quarter // 2) // quarter
    x = (turn - quarter * quadrant).astype(F32) * (2.0 * math.pi / PHASES)
    y = x * x
    s = x * (1.0 + y * (-1.0 / 6 + y * (1.0 / 120 + y * (-1.0 / 5040 + y * (1.0 / 362880)))))
    c = 1.0 + y * (-0.5 + y * (1.0 / 24 + y * (-1.0 / 720 + y * (1.0 / 40320 - y * (1.0 / 3628800)))))
    odd = quadrant & 1 == 1
    flip_c = (quadrant + 1) & 2 == 2
    flip_s = quadrant & 2 == 2
    cosine = jnp.where(odd, s, c)
    sine = jnp.where(odd, c, s)
    return jnp.where(flip_c, -cosine, cosine), jnp.where(flip_s, -sine, sine)


def fused(ni, nj, samples_hbm, table_hbm, index_hbm, out_ref, samples_ref, table_ref, index_ref, re_ref, im_ref, send_ref, recv_ref,
          steer_ref, x_ref, p_ref, load_sem, send_sem, recv_sem):
    nl, t_loc, q = 16, 16, 2 * CH_DEV
    antennas = ni * nl
    size = q * t_loc
    devices = ni * nj
    my_i, my_j = lax.axis_index("chan"), lax.axis_index("tm")
    me = my_i * nj + my_j

    barrier = pltpu.get_barrier_semaphore()

    def each_peer(body):
        def around(step, carry):
            ahead = my_i + step
            peer_i = jnp.where(ahead >= ni, ahead - ni, ahead)
            for peer_j in range(nj):
                body(peer_i, peer_j, nj * step + peer_j)
            return carry

        for shift in range(1, nj):
            ahead = my_j + shift
            body(my_i, jnp.where(ahead >= nj, ahead - nj, ahead), shift - 1)
        lax.fori_loop(1, ni, around, 0)

    def greet(peer_i, peer_j, slot):
        pl.semaphore_signal(barrier, inc=1, device_id=(peer_i, peer_j),
                            device_id_type=pl.DeviceIdType.MESH)

    each_peer(greet)

    loads = [pltpu.make_async_copy(src, dst, load_sem.at[i]) for i, (src, dst) in enumerate(
        [(table_hbm, table_ref), (samples_hbm.at[0], samples_ref.at[0]),
         (samples_hbm.at[1], samples_ref.at[1]), (index_hbm, index_ref)])]
    for load in loads:
        load.start()

    loads[0].wait()
    table = table_ref[...]
    half = table.shape[1] // 2
    loads[1].wait()
    first = dot(samples_ref[0], table)
    loads[2].wait()
    second = dot(samples_ref[1], table)
    re_ref[...] = first[:, :half] + second[:, half:]
    im_ref[...] = second[:, :half] - first[:, half:]
    parts = []
    for ref in (re_ref, im_ref):
        rows = [ref[pl.ds(t, nl, stride=t_loc), :] for t in range(t_loc)]
        parts.append(exchange_blocks(rows, ni, CH_DEV))
    blocks = jnp.concatenate(
        [jnp.concatenate([a, b], 1) for a, b in zip(*parts)], 0
    ).astype(BF16)
    src, dst = iota((size, size), 0), iota((size, size), 1)
    want = (dst // t_loc % 2) * (t_loc * CH_DEV) + (dst % t_loc) * CH_DEV + dst // (2 * t_loc)
    order = jnp.where(src == want, 1.0, 0.0).astype(BF16)
    send_ref[...] = dot(blocks, order).astype(BF16)

    pl.semaphore_wait(barrier, devices - 1)

    rows_of = lambda i: pl.ds(pl.multiple_of(i * nl, nl), nl)

    def copy_to(peer_i, peer_j, slot):
        return pltpu.make_async_remote_copy(
            src_ref=send_ref.at[rows_of(peer_i), :],
            dst_ref=recv_ref.at[my_j, rows_of(my_i), :],
            send_sem=send_sem.at[slot],
            recv_sem=recv_sem.at[me],
            device_id=(peer_i, peer_j),
            device_id_type=pl.DeviceIdType.MESH,
        )

    each_peer(lambda *peer: copy_to(*peer).start())
    mine = rows_of(my_i)
    recv_ref[my_j, mine, :] = send_ref[mine, :]

    loads[3].wait()
    cosine, sine = steering_parts(index_ref[...])
    steer_ref[0], steer_ref[1] = split(cosine)
    steer_ref[2], steer_ref[3] = split(sine)

    def arrive(peer_i, peer_j, slot):
        pltpu.make_async_remote_copy(
            src_ref=send_ref.at[mine, :],
            dst_ref=recv_ref.at[peer_j, rows_of(peer_i), :],
            send_sem=send_sem.at[slot],
            recv_sem=recv_sem.at[peer_i * nj + peer_j],
            device_id=(peer_i, peer_j),
            device_id_type=pl.DeviceIdType.MESH,
        ).wait_recv()

    each_peer(arrive)

    groups = size // LANES
    per = CH_DEV // groups
    cols = nj * LANES
    row_id, col_id = iota((cols, cols), 0), iota((cols, cols), 1)
    chan_of = lambda x: x // (2 * t_loc) % per
    same = chan_of(row_id) == chan_of(col_id)
    on_diag = row_id == col_id
    unit = jnp.where(on_diag, 1.0, 0.0).astype(BF16)
    turn_j = jnp.where(row_id == (col_id ^ t_loc), jnp.where(col_id & t_loc == 0, 1.0, -1.0), 0.0).astype(BF16)
    lane_chan = chan_of(iota((1, cols), 1))
    span = 2 * t_loc
    tiles = range(cols // span)

    def by_channel(values):
        return jnp.concatenate([jnp.broadcast_to(values[i % per], (span, cols)) for i in tiles], 0)

    for g in range(groups):
        z = jnp.concatenate([recv_ref[j, :, g * LANES : (g + 1) * LANES] for j in range(nj)], 1)
        zt = dot(unit, z, NT).astype(BF16)
        zj = dot(z, turn_j).astype(BF16)
        zjt = jnp.concatenate(
            [b for i in range(cols // span) for b in
             (zt[i * span + t_loc : (i + 1) * span], -zt[i * span : i * span + t_loc])], 0)
        gram = dot(zt, z) + dot(zjt, zj)
        pt = (dot(zt, steer_ref[0], NT) + dot(zt, steer_ref[1], NT)) + (
            dot(zjt, steer_ref[2], NT) + dot(zjt, steer_ref[3], NT))
        diagonal = jnp.where(on_diag, gram, 0.0)
        bounds, rhos = [], []
        for k in range(per):
            keep = jnp.where(lane_chan == k, 1.0, 0.0).astype(BF16)
            cov_re = dot(z * keep, zt)
            cov_im = dot(zj * keep, zt)
            power = cov_re * cov_re + cov_im * cov_im
            magnitude = power * lax.rsqrt(jnp.maximum(power, 1e-37))
            largest = jnp.max(jnp.sum(magnitude, axis=0, keepdims=True), axis=1, keepdims=True)
            trace = 0.0
            for j in range(nj):
                at = j * LANES + k * span
                trace += jnp.sum(jnp.sum(diagonal[at : at + span], axis=0, keepdims=True), axis=1, keepdims=True)
            load = (0.1 / antennas * 0.5) * trace
            bound = largest + load
            bounds.append(bound)
            rhos.append(1.0 - load / bound)
        sums = []
        for k in range(per):
            s, total = [], 1.0 + 0.0 * rhos[k]
            for m in range(TERMS):
                s.append(total)
                total = 1.0 + rhos[k] * total
            sums.append(s)
        inverse = [1.0 / b for b in bounds]
        x = jnp.where(same, gram, 0.0) * by_channel(inverse)
        r1 = jnp.where(on_diag, by_channel(rhos), 0.0) - x
        s1 = split(r1)
        r2 = dot3(s1, s1)
        s2 = split(r2)
        r3 = dot3(s2, s1)
        coef = lambda i: by_channel([sums[k][TERMS - 2 - i] for k in range(per)])
        tail = jnp.where(on_diag, coef(3), 0.0) + coef(4) * r1 + coef(5) * r2 + coef(6) * r3
        poly = (jnp.where(on_diag, coef(0), 0.0) + coef(1) * r1 + coef(2) * r2) + dot3(split(r3), split(tail))
        vt = dot3(split(poly), split(pt))
        product = pt * vt
        x_ref[...] = x
        p_ref[...] = pt
        own = pl.ds(pl.multiple_of(my_j * LANES, LANES), LANES)
        back = dot3(split(x_ref[own, :]), split(vt))
        mine_p = p_ref[own, :]
        for k in range(per):
            at = k * span
            energy = 0.0
            for j in range(nj):
                low = j * LANES + at
                energy += jnp.sum(product[low : low + span], axis=0, keepdims=True)
            whole = sums[k][TERMS - 1]
            response = antennas * whole - energy * inverse[k]
            factor = lax.rsqrt(response) * lax.rsqrt(bounds[k] * (1.0 / (nj * t_loc)))
            beam = (whole * mine_p[at : at + span] - back[at : at + span]) * factor
            beam = beam.astype(BF16)
            out_ref[0, g * per + k] = beam[:t_loc]
            out_ref[1, g * per + k] = beam[t_loc:]

    each_peer(lambda *peer: copy_to(*peer).wait_send())


def fused_local(ni, nj, samples, steer_index):
    _, nl, t_loc, _ = samples.shape
    beams, antennas = steer_index.shape
    size = 2 * CH_DEV * t_loc
    cols = nj * LANES
    vmem = pl.BlockSpec(memory_space=pltpu.VMEM)
    table = jnp.asarray(taper_table(CH_DEV * ni))
    out = pl.pallas_call(
        functools.partial(fused, ni, nj),
        out_shape=pltpu.VMEM((2, CH_DEV, t_loc, beams), BF16),
        in_specs=[pl.BlockSpec(memory_space=pl.ANY)] * 3,
        out_specs=vmem,
        scratch_shapes=[
            pltpu.VMEM((2, nl * t_loc, C), BF16),
            pltpu.VMEM(table.shape, BF16),
            pltpu.VMEM((beams, antennas), jnp.int32),
            pltpu.VMEM((nl * t_loc, CH_DEV * ni), F32),
            pltpu.VMEM((nl * t_loc, CH_DEV * ni), F32),
            pltpu.VMEM((antennas, size), BF16),
            pltpu.VMEM((nj, antennas, size), BF16),
            pltpu.VMEM((4, beams, antennas), BF16),
            pltpu.VMEM((cols, cols), F32),
            pltpu.VMEM((cols, beams), F32),
            pltpu.SemaphoreType.DMA((4,)),
            pltpu.SemaphoreType.DMA((ni * nj,)),
            pltpu.SemaphoreType.DMA((ni * nj,)),
        ],
        compiler_params=pltpu.CompilerParams(collective_id=0, has_side_effects=True),
    )(samples.reshape(2, nl * t_loc, C), table, steer_index)
    return jnp.transpose(out, (0, 1, 3, 2))


def choose(ni, nj, samples, steer_index):
    _, nl, t_loc, _ = samples.shape
    beams, antennas = steer_index.shape
    tiled = nl == 16 and t_loc == 16 and CH_DEV * ni == LANES and antennas == nl * ni
    if tiled and nj * LANES == antennas:
        return fused_local(ni, nj, samples, steer_index)
    return local(samples, steer_index)


def solution(mesh):
    return jax.shard_map(
        functools.partial(choose, mesh.shape["chan"], mesh.shape["tm"]),
        mesh=mesh,
        in_specs=(P(None, "chan", "tm", None), P()),
        out_specs=P(None, "chan", None, "tm"),
        check_vma=False,
    )
```

```python
import functools
import itertools
import math

import jax
import jax.numpy as jnp
import numpy as np
from jax import lax
from jax.experimental import pallas as pl
from jax.experimental.pallas import tpu as pltpu
from jax.sharding import PartitionSpec as P

C = 1024
PHASES = 256
CH_DEV = 8
ITERS = 3
TERMS = 2**ITERS
LANES = 128


HIGHEST = lax.Precision.HIGHEST
F32 = jnp.float32
BF16 = jnp.bfloat16
NT = (((1,), (1,)), ((), ()))


def transform_table(channels_all):
    offset = (C - channels_all) // 2
    channel_number = jnp.arange(channels_all, dtype=jnp.int32) + offset
    sample_number = jnp.arange(C, dtype=jnp.int32)
    phase_turns = channel_number[:, None] * sample_number[None, :] % C
    phase_angle = 2.0 * math.pi / C * phase_turns.astype(jnp.float32)
    window_taper = (
        0.5 - 0.5 * jnp.cos(2.0 * math.pi / C * sample_number.astype(jnp.float32))
    ) / math.sqrt(C)
    cosine = window_taper[None, :] * jnp.cos(phase_angle)
    sine_part = window_taper[None, :] * jnp.sin(phase_angle)
    coefficients = jnp.stack(
        [jnp.stack([cosine, sine_part], 1), jnp.stack([-sine_part, cosine], 1)], 0
    )
    return coefficients.astype(jnp.bfloat16)


def complex_product(left_real, left_imag, right_real, right_imag):
    real_part = jnp.dot(left_real, right_real, precision=HIGHEST) - jnp.dot(
        left_imag, right_imag, precision=HIGHEST
    )
    imag_part = jnp.dot(left_real, right_imag, precision=HIGHEST) + jnp.dot(
        left_imag, right_real, precision=HIGHEST
    )
    return (real_part, imag_part)


def invert_loaded(covariance_real, covariance_imag):
    matrix_order = covariance_real.shape[0]
    loading = 0.1 * jnp.mean(jnp.diagonal(covariance_real))
    identity = jnp.eye(matrix_order, dtype=jnp.float32)
    loaded = covariance_real + loading * identity
    magnitude = jnp.sqrt(loaded * loaded + covariance_imag * covariance_imag)
    largest = jnp.max(jnp.sum(magnitude, axis=1))

    def iterate(counter, state):
        approx_real, approx_imag = state
        image_real, image_imag = complex_product(loaded, covariance_imag, approx_real, approx_imag)
        square_real, square_imag = complex_product(approx_real, approx_imag, image_real, image_imag)
        return (2.0 * approx_real - square_real, 2.0 * approx_imag - square_imag)

    start_state = (identity / largest, jnp.zeros_like(identity))
    return lax.fori_loop(0, ITERS, iterate, start_state)


def form_weights(covariance_real, covariance_imag, steer_real, steer_imag):
    inverse_real, inverse_imag = invert_loaded(covariance_real, covariance_imag)
    gain_real, gain_imag = complex_product(inverse_real, inverse_imag, steer_real, steer_imag)
    response = jnp.sum(steer_real * gain_real + steer_imag * gain_imag, axis=0)
    factor = lax.rsqrt(response)
    return ((gain_real * factor).astype(jnp.bfloat16), (gain_imag * factor).astype(jnp.bfloat16))


def weights_stacked(covariance_real, covariance_imag, steer_real, steer_imag):
    weight_real, weight_imag = jax.vmap(form_weights, in_axes=(0, 0, None, None))(
        covariance_real, covariance_imag, steer_real, steer_imag
    )
    return jnp.stack([weight_real, weight_imag], 1)


def steering(steer_index):
    phase_angle = 2.0 * math.pi / PHASES * steer_index.astype(jnp.float32)
    return (jnp.cos(phase_angle).T, jnp.sin(phase_angle).T)


def apply_beams(weight_pair, spectrum):
    real_weight = weight_pair[:, 0]
    imag_weight = weight_pair[:, 1]
    beam_real = jnp.einsum(
        "knb,kns->kbs", real_weight, spectrum[0], preferred_element_type=jnp.float32
    ) + jnp.einsum("knb,kns->kbs", imag_weight, spectrum[1], preferred_element_type=jnp.float32)
    beam_imag = jnp.einsum(
        "knb,kns->kbs", real_weight, spectrum[1], preferred_element_type=jnp.float32
    ) - jnp.einsum("knb,kns->kbs", imag_weight, spectrum[0], preferred_element_type=jnp.float32)
    return jnp.stack([beam_real, beam_imag], 0).astype(jnp.bfloat16)


def local(samples, steer_index):
    channels_all = CH_DEV * lax.axis_size("chan")
    coefficients = transform_table(channels_all)
    spectra = lax.dot_general(
        coefficients, samples, (((2, 3), (0, 3)), ((), ())), preferred_element_type=jnp.float32
    ).astype(jnp.bfloat16)
    steer_real, steer_imag = steering(steer_index)
    turned = lax.all_to_all(
        lax.all_to_all(spectra, "chan", split_axis=1, concat_axis=2, tiled=True),
        "tm",
        split_axis=1,
        concat_axis=3,
        tiled=True,
    )
    outer_sums = jnp.einsum("ikns,jkms->kinjm", turned, turned, preferred_element_type=jnp.float32)
    snapshots = turned.shape[3]
    covariance_real = (outer_sums[:, 0, :, 0, :] + outer_sums[:, 1, :, 1, :]) / snapshots
    covariance_imag = (outer_sums[:, 1, :, 0, :] - outer_sums[:, 0, :, 1, :]) / snapshots
    weight_pair = weights_stacked(covariance_real, covariance_imag, steer_real, steer_imag)
    local_beams = apply_beams(weight_pair, turned)
    return lax.all_to_all(local_beams, "tm", split_axis=3, concat_axis=1, tiled=True)


def taper_table(channels_all):
    offset = (C - channels_all) // 2
    channel = np.arange(channels_all) + offset
    sample = np.arange(C)
    angle = 2.0 * math.pi / C * (channel[None, :] * sample[:, None] % C)
    taper = (0.5 - 0.5 * np.cos(2.0 * math.pi / C * sample)) / math.sqrt(C)
    both = np.concatenate([taper[:, None] * np.cos(angle), taper[:, None] * np.sin(angle)], 1)
    return both.astype(np.float32).astype(BF16)


def iota(shape, axis):
    return lax.broadcasted_iota(jnp.int32, shape, axis)


def dot(a, b, dims=(((1,), (0,)), ((), ()))):
    return lax.dot_general(a, b, dims, preferred_element_type=F32)


def split(x):
    high = x.astype(BF16)
    return high, (x - high.astype(F32)).astype(BF16)


def dot3(a, b):
    (ah, al), (bh, bl) = a, b
    return dot(ah, bh) + (dot(ah, bl) + dot(al, bh))


def exchange_blocks(rows, count, width):
    lane = iota(rows[0].shape, 1)
    total = count * width
    step = count // 2
    while step:
        low = (lane // width) & step == 0
        done = list(rows)
        for a in range(count):
            if a & step:
                continue
            b = a + step
            up = pltpu.roll(rows[b], step * width, 1)
            down = pltpu.roll(rows[a], total - step * width, 1)
            done[a] = jnp.where(low, rows[a], up)
            done[b] = jnp.where(low, down, rows[b])
        rows = done
        step //= 2
    return rows


def steering_parts(index):
    turn = index & (PHASES - 1)
    quarter = PHASES // 4
    quadrant = (turn + quarter // 2) // quarter
    x = (turn - quarter * quadrant).astype(F32) * (2.0 * math.pi / PHASES)
    y = x * x
    s = x * (1.0 + y * (-1.0 / 6 + y * (1.0 / 120 + y * (-1.0 / 5040 + y * (1.0 / 362880)))))
    c = 1.0 + y * (-0.5 + y * (1.0 / 24 + y * (-1.0 / 720 + y * (1.0 / 40320 - y * (1.0 / 3628800)))))
    odd = quadrant & 1 == 1
    flip_c = (quadrant + 1) & 2 == 2
    flip_s = quadrant & 2 == 2
    cosine = jnp.where(odd, s, c)
    sine = jnp.where(odd, c, s)
    return jnp.where(flip_c, -cosine, cosine), jnp.where(flip_s, -sine, sine)


def fused(ni, nj, samples_hbm, table_hbm, index_hbm, out_ref, samples_ref, table_ref, index_ref, re_ref,
          im_ref, send_ref, recv_ref, steer_ref, load_sem, send_sem, recv_sem):
    nl, t_loc, q = 16, 16, 2 * CH_DEV
    antennas = ni * nl
    size = q * t_loc
    my_i, my_j = lax.axis_index("chan"), lax.axis_index("tm")
    other_j = 1 - my_j

    barrier = pltpu.get_barrier_semaphore()

    def after(step):
        ahead = my_i + step
        return jnp.where(ahead >= ni, ahead - ni, ahead)

    def around(body):
        lax.fori_loop(1, ni, lambda step, carry: (body(step), carry)[1], 0)

    def greet(peer_i, peer_j):
        pl.semaphore_signal(barrier, inc=1, device_id=(peer_i, peer_j),
                            device_id_type=pl.DeviceIdType.MESH)

    greet(my_i, other_j)

    def greet_both(step):
        greet(after(step), my_j)
        greet(after(step), other_j)

    around(greet_both)

    loads = [pltpu.make_async_copy(src, dst, load_sem.at[i]) for i, (src, dst) in enumerate(
        [(table_hbm, table_ref), (samples_hbm.at[0], samples_ref.at[0]),
         (samples_hbm.at[1], samples_ref.at[1]), (index_hbm, index_ref)])]
    for load in loads:
        load.start()

    loads[0].wait()
    table = table_ref[...]
    half = table.shape[1] // 2
    loads[1].wait()
    first = dot(samples_ref[0], table)
    loads[2].wait()
    second = dot(samples_ref[1], table)
    re_ref[...] = first[:, :half] + second[:, half:]
    im_ref[...] = second[:, :half] - first[:, half:]
    parts = []
    for ref in (re_ref, im_ref):
        rows = [ref[pl.ds(t, nl, stride=t_loc), :] for t in range(t_loc)]
        parts.append(exchange_blocks(rows, ni, CH_DEV))
    blocks = jnp.concatenate(
        [jnp.concatenate([a, b], 1) for a, b in zip(*parts)], 0
    ).astype(BF16)
    src, dst = iota((size, size), 0), iota((size, size), 1)
    want = (dst // t_loc % 2) * (t_loc * CH_DEV) + (dst % t_loc) * CH_DEV + dst // (2 * t_loc)
    order = jnp.where(src == want, 1.0, 0.0).astype(BF16)
    send_ref[...] = dot(blocks, order).astype(BF16)

    pl.semaphore_wait(barrier, ni * nj - 1)

    rows_of = lambda i: pl.ds(pl.multiple_of(i * nl, nl), nl)
    mine = rows_of(my_i)

    def block_copy(step, origin, plane):
        peer = after(step)
        return pltpu.make_async_remote_copy(
            src_ref=send_ref.at[rows_of(peer), :],
            dst_ref=recv_ref.at[plane, rows_of(origin), :],
            send_sem=send_sem.at[plane, step],
            recv_sem=recv_sem.at[plane, origin],
            device_id=(peer, other_j if plane else my_j),
            device_id_type=pl.DeviceIdType.MESH,
        )

    def send(step):
        block_copy(step, my_i, 0).start()
        block_copy(step, my_i, 1).start()

    block_copy(0, my_i, 1).start()
    around(send)
    recv_ref[0, mine, :] = send_ref[mine, :]

    loads[3].wait()
    cosine, sine = steering_parts(index_ref[...])
    steer_ref[0], steer_ref[1] = split(cosine)
    steer_ref[2], steer_ref[3] = split(sine)

    span = 2 * t_loc
    row_id, col_id = iota((size, size), 0), iota((size, size), 1)
    on_diag = row_id == col_id
    unit = jnp.where(on_diag, 1.0, 0.0).astype(BF16)
    turn_j = jnp.where(row_id == (col_id ^ t_loc), jnp.where(col_id & t_loc == 0, 1.0, -1.0), 0.0).astype(BF16)

    def prepare(plane):
        z = recv_ref[plane]
        zt = dot(unit, z, NT).astype(BF16)
        zj = dot(z, turn_j).astype(BF16)
        zjt = jnp.concatenate(
            [b for i in range(size // span) for b in
             (zt[i * span + t_loc : (i + 1) * span], -zt[i * span : i * span + t_loc])], 0)
        pt = (dot(zt, steer_ref[0], NT) + dot(zt, steer_ref[1], NT)) + (
            dot(zjt, steer_ref[2], NT) + dot(zjt, steer_ref[3], NT))
        return z, zt, zj, zjt, pt

    around(lambda step: block_copy(step, after(step), 0).wait_recv())
    planes = [prepare(0)]
    block_copy(0, my_i, 1).wait_recv()
    around(lambda step: block_copy(step, after(step), 1).wait_recv())
    planes.append(prepare(1))

    groups = size // LANES
    per = CH_DEV // groups
    cols = nj * LANES
    chan_of = lambda x: x // span % per
    same = chan_of(row_id) == chan_of(col_id)
    lane_chan = chan_of(iota((1, cols), 1))

    def by_channel(values):
        return jnp.concatenate([jnp.broadcast_to(values[i % per], (span, cols)) for i in range(cols // span)], 0)

    def group_steps(g):
        cut = slice(g * LANES, (g + 1) * LANES)
        z = jnp.concatenate([p[0][:, cut] for p in planes], 1)
        zj = jnp.concatenate([p[2][:, cut] for p in planes], 1)
        zt, zjt, pt = (jnp.concatenate([p[i][cut] for p in planes], 0) for i in (1, 3, 4))
        gram = dot(zt, z) + dot(zjt, zj)
        yield
        diagonal = jnp.where(on_diag, gram, 0.0)
        bounds, rhos = [], []
        for k in range(per):
            yield
            keep = jnp.where(lane_chan == k, 1.0, 0.0).astype(BF16)
            cov_re = dot(z * keep, zt)
            cov_im = dot(zj * keep, zt)
            power = cov_re * cov_re + cov_im * cov_im
            magnitude = power * lax.rsqrt(jnp.maximum(power, 1e-37))
            largest = jnp.max(jnp.sum(magnitude, axis=0, keepdims=True), axis=1, keepdims=True)
            trace = 0.0
            for j in range(nj):
                at = j * LANES + k * span
                trace += jnp.sum(jnp.sum(diagonal[at : at + span], axis=0, keepdims=True), axis=1, keepdims=True)
            load = (0.1 / antennas * 0.5) * trace
            bound = largest + load
            bounds.append(bound)
            rhos.append(1.0 - load / bound)
        yield
        sums = []
        for k in range(per):
            s, total = [], 1.0 + 0.0 * rhos[k]
            for m in range(TERMS):
                s.append(total)
                total = 1.0 + rhos[k] * total
            sums.append(s)
        inverse = [1.0 / b for b in bounds]
        x = jnp.where(same, gram, 0.0) * by_channel(inverse)
        r1 = jnp.where(on_diag, by_channel(rhos), 0.0) - x
        s1 = split(r1)
        yield
        r2 = dot3(s1, s1)
        yield
        r3 = dot3(split(r2), s1)
        coef = lambda i: by_channel([sums[k][TERMS - 2 - i] for k in range(per)])
        yield
        tail = jnp.where(on_diag, coef(3), 0.0) + coef(4) * r1 + coef(5) * r2 + coef(6) * r3
        poly = (jnp.where(on_diag, coef(0), 0.0) + coef(1) * r1 + coef(2) * r2) + dot3(split(r3), split(tail))
        yield
        vt = dot3(split(poly), split(pt))
        yield
        product = pt * vt
        back = dot3(split(x[:LANES]), split(vt))
        for k in range(per):
            at = k * span
            energy = 0.0
            for j in range(nj):
                low = j * LANES + at
                energy += jnp.sum(product[low : low + span], axis=0, keepdims=True)
            whole = sums[k][TERMS - 1]
            response = antennas * whole - energy * inverse[k]
            factor = lax.rsqrt(response) * lax.rsqrt(bounds[k] * (1.0 / (nj * t_loc)))
            beam = (whole * pt[at : at + span] - back[at : at + span]) * factor
            beam = beam.astype(BF16)
            out_ref[0, g * per + k] = beam[:t_loc]
            out_ref[1, g * per + k] = beam[t_loc:]

    for _ in itertools.zip_longest(*[group_steps(g) for g in range(groups)]):
        pass

    block_copy(0, my_i, 1).wait_send()

    def drain(step):
        block_copy(step, my_i, 0).wait_send()
        block_copy(step, my_i, 1).wait_send()

    around(drain)


def fused_local(ni, nj, samples, steer_index):
    _, nl, t_loc, _ = samples.shape
    beams, antennas = steer_index.shape
    size = 2 * CH_DEV * t_loc
    vmem = pl.BlockSpec(memory_space=pltpu.VMEM)
    table = jnp.asarray(taper_table(CH_DEV * ni))
    out = pl.pallas_call(
        functools.partial(fused, ni, nj),
        out_shape=pltpu.VMEM((2, CH_DEV, t_loc, beams), BF16),
        in_specs=[pl.BlockSpec(memory_space=pl.ANY)] * 3,
        out_specs=vmem,
        scratch_shapes=[
            pltpu.VMEM((2, nl * t_loc, C), BF16),
            pltpu.VMEM(table.shape, BF16),
            pltpu.VMEM((beams, antennas), jnp.int32),
            pltpu.VMEM((nl * t_loc, CH_DEV * ni), F32),
            pltpu.VMEM((nl * t_loc, CH_DEV * ni), F32),
            pltpu.VMEM((antennas, size), BF16),
            pltpu.VMEM((nj, antennas, size), BF16),
            pltpu.VMEM((4, beams, antennas), BF16),
            pltpu.SemaphoreType.DMA((4,)),
            pltpu.SemaphoreType.DMA((nj, ni)),
            pltpu.SemaphoreType.DMA((nj, ni)),
        ],
        compiler_params=pltpu.CompilerParams(collective_id=0, has_side_effects=True),
    )(samples.reshape(2, nl * t_loc, C), table, steer_index)
    return jnp.transpose(out, (0, 1, 3, 2))


def choose(ni, nj, samples, steer_index):
    _, nl, t_loc, _ = samples.shape
    beams, antennas = steer_index.shape
    tiled = nl == 16 and t_loc == 16 and CH_DEV * ni == LANES and antennas == nl * ni
    if tiled and nj == 2:
        return fused_local(ni, nj, samples, steer_index)
    return local(samples, steer_index)


def solution(mesh):
    return jax.shard_map(
        functools.partial(choose, mesh.shape["chan"], mesh.shape["tm"]),
        mesh=mesh,
        in_specs=(P(None, "chan", "tm", None), P()),
        out_specs=P(None, "chan", None, "tm"),
        check_vma=False,
    )
```

```python
import functools
import itertools
import math

import jax
import jax.numpy as jnp
import numpy as np
from jax import lax
from jax.experimental import pallas as pl
from jax.experimental.pallas import tpu as pltpu
from jax.sharding import PartitionSpec as P

C = 1024
PHASES = 256
CH_DEV = 8
ITERS = 3
TERMS = 2**ITERS
LANES = 128


HIGHEST = lax.Precision.HIGHEST
F32 = jnp.float32
BF16 = jnp.bfloat16
NT = (((1,), (1,)), ((), ()))


def transform_table(channels_all):
    offset = (C - channels_all) // 2
    channel_number = jnp.arange(channels_all, dtype=jnp.int32) + offset
    sample_number = jnp.arange(C, dtype=jnp.int32)
    phase_turns = channel_number[:, None] * sample_number[None, :] % C
    phase_angle = 2.0 * math.pi / C * phase_turns.astype(jnp.float32)
    window_taper = (
        0.5 - 0.5 * jnp.cos(2.0 * math.pi / C * sample_number.astype(jnp.float32))
    ) / math.sqrt(C)
    cosine = window_taper[None, :] * jnp.cos(phase_angle)
    sine_part = window_taper[None, :] * jnp.sin(phase_angle)
    coefficients = jnp.stack(
        [jnp.stack([cosine, sine_part], 1), jnp.stack([-sine_part, cosine], 1)], 0
    )
    return coefficients.astype(jnp.bfloat16)


def complex_product(left_real, left_imag, right_real, right_imag):
    real_part = jnp.dot(left_real, right_real, precision=HIGHEST) - jnp.dot(
        left_imag, right_imag, precision=HIGHEST
    )
    imag_part = jnp.dot(left_real, right_imag, precision=HIGHEST) + jnp.dot(
        left_imag, right_real, precision=HIGHEST
    )
    return (real_part, imag_part)


def invert_loaded(covariance_real, covariance_imag):
    matrix_order = covariance_real.shape[0]
    loading = 0.1 * jnp.mean(jnp.diagonal(covariance_real))
    identity = jnp.eye(matrix_order, dtype=jnp.float32)
    loaded = covariance_real + loading * identity
    magnitude = jnp.sqrt(loaded * loaded + covariance_imag * covariance_imag)
    largest = jnp.max(jnp.sum(magnitude, axis=1))

    def iterate(counter, state):
        approx_real, approx_imag = state
        image_real, image_imag = complex_product(loaded, covariance_imag, approx_real, approx_imag)
        square_real, square_imag = complex_product(approx_real, approx_imag, image_real, image_imag)
        return (2.0 * approx_real - square_real, 2.0 * approx_imag - square_imag)

    start_state = (identity / largest, jnp.zeros_like(identity))
    return lax.fori_loop(0, ITERS, iterate, start_state)


def form_weights(covariance_real, covariance_imag, steer_real, steer_imag):
    inverse_real, inverse_imag = invert_loaded(covariance_real, covariance_imag)
    gain_real, gain_imag = complex_product(inverse_real, inverse_imag, steer_real, steer_imag)
    response = jnp.sum(steer_real * gain_real + steer_imag * gain_imag, axis=0)
    factor = lax.rsqrt(response)
    return ((gain_real * factor).astype(jnp.bfloat16), (gain_imag * factor).astype(jnp.bfloat16))


def weights_stacked(covariance_real, covariance_imag, steer_real, steer_imag):
    weight_real, weight_imag = jax.vmap(form_weights, in_axes=(0, 0, None, None))(
        covariance_real, covariance_imag, steer_real, steer_imag
    )
    return jnp.stack([weight_real, weight_imag], 1)


def steering(steer_index):
    phase_angle = 2.0 * math.pi / PHASES * steer_index.astype(jnp.float32)
    return (jnp.cos(phase_angle).T, jnp.sin(phase_angle).T)


def apply_beams(weight_pair, spectrum):
    real_weight = weight_pair[:, 0]
    imag_weight = weight_pair[:, 1]
    beam_real = jnp.einsum(
        "knb,kns->kbs", real_weight, spectrum[0], preferred_element_type=jnp.float32
    ) + jnp.einsum("knb,kns->kbs", imag_weight, spectrum[1], preferred_element_type=jnp.float32)
    beam_imag = jnp.einsum(
        "knb,kns->kbs", real_weight, spectrum[1], preferred_element_type=jnp.float32
    ) - jnp.einsum("knb,kns->kbs", imag_weight, spectrum[0], preferred_element_type=jnp.float32)
    return jnp.stack([beam_real, beam_imag], 0).astype(jnp.bfloat16)


def local(samples, steer_index):
    channels_all = CH_DEV * lax.axis_size("chan")
    coefficients = transform_table(channels_all)
    spectra = lax.dot_general(
        coefficients, samples, (((2, 3), (0, 3)), ((), ())), preferred_element_type=jnp.float32
    ).astype(jnp.bfloat16)
    steer_real, steer_imag = steering(steer_index)
    turned = lax.all_to_all(
        lax.all_to_all(spectra, "chan", split_axis=1, concat_axis=2, tiled=True),
        "tm",
        split_axis=1,
        concat_axis=3,
        tiled=True,
    )
    outer_sums = jnp.einsum("ikns,jkms->kinjm", turned, turned, preferred_element_type=jnp.float32)
    snapshots = turned.shape[3]
    covariance_real = (outer_sums[:, 0, :, 0, :] + outer_sums[:, 1, :, 1, :]) / snapshots
    covariance_imag = (outer_sums[:, 1, :, 0, :] - outer_sums[:, 0, :, 1, :]) / snapshots
    weight_pair = weights_stacked(covariance_real, covariance_imag, steer_real, steer_imag)
    local_beams = apply_beams(weight_pair, turned)
    return lax.all_to_all(local_beams, "tm", split_axis=3, concat_axis=1, tiled=True)


def taper_table(channels_all):
    offset = (C - channels_all) // 2
    channel = np.arange(channels_all) + offset
    sample = np.arange(C)
    angle = 2.0 * math.pi / C * (channel[None, :] * sample[:, None] % C)
    taper = (0.5 - 0.5 * np.cos(2.0 * math.pi / C * sample)) / math.sqrt(C)
    both = np.concatenate([taper[:, None] * np.cos(angle), taper[:, None] * np.sin(angle)], 1)
    return both.astype(np.float32).astype(BF16)


def iota(shape, axis):
    return lax.broadcasted_iota(jnp.int32, shape, axis)


def dot(a, b, dims=(((1,), (0,)), ((), ()))):
    return lax.dot_general(a, b, dims, preferred_element_type=F32)


def split(x):
    high = x.astype(BF16)
    return high, (x - high.astype(F32)).astype(BF16)


def dot3(a, b):
    (ah, al), (bh, bl) = a, b
    return dot(ah, bh) + (dot(ah, bl) + dot(al, bh))


def exchange_blocks(rows, count, width):
    lane = iota(rows[0].shape, 1)
    total = count * width
    step = count // 2
    while step:
        low = (lane // width) & step == 0
        done = list(rows)
        for a in range(count):
            if a & step:
                continue
            b = a + step
            up = pltpu.roll(rows[b], step * width, 1)
            down = pltpu.roll(rows[a], total - step * width, 1)
            done[a] = jnp.where(low, rows[a], up)
            done[b] = jnp.where(low, down, rows[b])
        rows = done
        step //= 2
    return rows


def steering_parts(index):
    turn = index & (PHASES - 1)
    quarter = PHASES // 4
    quadrant = (turn + quarter // 2) // quarter
    x = (turn - quarter * quadrant).astype(F32) * (2.0 * math.pi / PHASES)
    y = x * x
    s = x * (1.0 + y * (-1.0 / 6 + y * (1.0 / 120 + y * (-1.0 / 5040 + y * (1.0 / 362880)))))
    c = 1.0 + y * (-0.5 + y * (1.0 / 24 + y * (-1.0 / 720 + y * (1.0 / 40320 - y * (1.0 / 3628800)))))
    odd = quadrant & 1 == 1
    flip_c = (quadrant + 1) & 2 == 2
    flip_s = quadrant & 2 == 2
    cosine = jnp.where(odd, s, c)
    sine = jnp.where(odd, c, s)
    return jnp.where(flip_c, -cosine, cosine), jnp.where(flip_s, -sine, sine)


def fused(ni, nj, samples_hbm, table_hbm, index_hbm, out_ref, samples_ref, table_ref, index_ref, re_ref,
          im_ref, send_ref, recv_ref, steer_ref, load_sem, send_sem, recv_sem):
    nl, t_loc, q = 16, 16, 2 * CH_DEV
    antennas = ni * nl
    size = q * t_loc
    my_i, my_j = lax.axis_index("chan"), lax.axis_index("tm")
    other_j = 1 - my_j

    barrier = pltpu.get_barrier_semaphore()

    def after(step):
        ahead = my_i + step
        return jnp.where(ahead >= ni, ahead - ni, ahead)

    def around(body):
        lax.fori_loop(1, ni, lambda step, carry: (body(step), carry)[1], 0)

    def greet(peer_i, peer_j):
        pl.semaphore_signal(barrier, inc=1, device_id=(peer_i, peer_j),
                            device_id_type=pl.DeviceIdType.MESH)

    greet(my_i, other_j)

    def greet_both(step):
        greet(after(step), my_j)
        greet(after(step), other_j)

    around(greet_both)

    loads = [pltpu.make_async_copy(src, dst, load_sem.at[i]) for i, (src, dst) in enumerate(
        [(table_hbm, table_ref), (samples_hbm.at[0], samples_ref.at[0]),
         (samples_hbm.at[1], samples_ref.at[1]), (index_hbm, index_ref)])]
    for load in loads:
        load.start()

    loads[0].wait()
    table = table_ref[...]
    half = table.shape[1] // 2
    loads[1].wait()
    first = dot(samples_ref[0], table)
    loads[2].wait()
    second = dot(samples_ref[1], table)
    re_ref[...] = first[:, :half] + second[:, half:]
    im_ref[...] = second[:, :half] - first[:, half:]
    parts = []
    for ref in (re_ref, im_ref):
        rows = [ref[pl.ds(t, nl, stride=t_loc), :] for t in range(t_loc)]
        parts.append(exchange_blocks(rows, ni, CH_DEV))
    blocks = jnp.concatenate(
        [jnp.concatenate([a, b], 1) for a, b in zip(*parts)], 0
    ).astype(BF16)
    src, dst = iota((size, size), 0), iota((size, size), 1)
    want = (dst // t_loc % 2) * (t_loc * CH_DEV) + (dst % t_loc) * CH_DEV + dst // (2 * t_loc)
    order = jnp.where(src == want, 1.0, 0.0).astype(BF16)
    send_ref[...] = dot(blocks, order).astype(BF16)

    pl.semaphore_wait(barrier, ni * nj - 1)

    rows_of = lambda i: pl.ds(pl.multiple_of(i * nl, nl), nl)
    mine = rows_of(my_i)

    def block_copy(step, origin, plane):
        peer = after(step)
        return pltpu.make_async_remote_copy(
            src_ref=send_ref.at[rows_of(peer), :],
            dst_ref=recv_ref.at[plane, rows_of(origin), :],
            send_sem=send_sem,
            recv_sem=recv_sem.at[plane],
            device_id=(peer, other_j if plane else my_j),
            device_id_type=pl.DeviceIdType.MESH,
        )

    def send(step):
        block_copy(step, my_i, 0).start()
        block_copy(step, my_i, 1).start()

    block_copy(0, my_i, 1).start()
    around(send)
    recv_ref[0, mine, :] = send_ref[mine, :]

    loads[3].wait()
    cosine, sine = steering_parts(index_ref[...])
    steer_ref[0], steer_ref[1] = split(cosine)
    steer_ref[2], steer_ref[3] = split(sine)

    span = 2 * t_loc
    row_id, col_id = iota((size, size), 0), iota((size, size), 1)
    on_diag = row_id == col_id
    unit = jnp.where(on_diag, 1.0, 0.0).astype(BF16)
    turn_j = jnp.where(row_id == (col_id ^ t_loc), jnp.where(col_id & t_loc == 0, 1.0, -1.0), 0.0).astype(BF16)

    def prepare(plane):
        z = recv_ref[plane]
        zt = dot(unit, z, NT).astype(BF16)
        zj = dot(z, turn_j).astype(BF16)
        zjt = jnp.concatenate(
            [b for i in range(size // span) for b in
             (zt[i * span + t_loc : (i + 1) * span], -zt[i * span : i * span + t_loc])], 0)
        pt = (dot(zt, steer_ref[0], NT) + dot(zt, steer_ref[1], NT)) + (
            dot(zjt, steer_ref[2], NT) + dot(zjt, steer_ref[3], NT))
        return z, zt, zj, zjt, pt

    def sized(ref, plane):
        return pltpu.make_async_remote_copy(
            src_ref=ref, dst_ref=ref, send_sem=send_sem, recv_sem=recv_sem.at[plane],
            device_id=(my_i, other_j), device_id_type=pl.DeviceIdType.MESH)

    sized(recv_ref.at[0, : antennas - nl], 0).wait_recv()
    planes = [prepare(0)]
    sized(recv_ref.at[1], 1).wait_recv()
    planes.append(prepare(1))

    groups = size // LANES
    per = CH_DEV // groups
    cols = nj * LANES
    chan_of = lambda x: x // span % per
    same = chan_of(row_id) == chan_of(col_id)
    lane_chan = chan_of(iota((1, cols), 1))

    def by_channel(values):
        return jnp.concatenate([jnp.broadcast_to(values[i % per], (span, cols)) for i in range(cols // span)], 0)

    def group_steps(g):
        cut = slice(g * LANES, (g + 1) * LANES)
        z = jnp.concatenate([p[0][:, cut] for p in planes], 1)
        zj = jnp.concatenate([p[2][:, cut] for p in planes], 1)
        zt, zjt, pt = (jnp.concatenate([p[i][cut] for p in planes], 0) for i in (1, 3, 4))
        gram = dot(zt, z) + dot(zjt, zj)
        yield
        diagonal = jnp.where(on_diag, gram, 0.0)
        bounds, rhos = [], []
        for k in range(per):
            yield
            keep = jnp.where(lane_chan == k, 1.0, 0.0).astype(BF16)
            cov_re = dot(z * keep, zt)
            cov_im = dot(zj * keep, zt)
            power = cov_re * cov_re + cov_im * cov_im
            magnitude = power * lax.rsqrt(jnp.maximum(power, 1e-37))
            largest = jnp.max(jnp.sum(magnitude, axis=0, keepdims=True), axis=1, keepdims=True)
            trace = 0.0
            for j in range(nj):
                at = j * LANES + k * span
                trace += jnp.sum(jnp.sum(diagonal[at : at + span], axis=0, keepdims=True), axis=1, keepdims=True)
            load = (0.1 / antennas * 0.5) * trace
            bound = largest + load
            bounds.append(bound)
            rhos.append(1.0 - load / bound)
        yield
        sums = []
        for k in range(per):
            s, total = [], 1.0 + 0.0 * rhos[k]
            for m in range(TERMS):
                s.append(total)
                total = 1.0 + rhos[k] * total
            sums.append(s)
        inverse = [1.0 / b for b in bounds]
        x = jnp.where(same, gram, 0.0) * by_channel(inverse)
        r1 = jnp.where(on_diag, by_channel(rhos), 0.0) - x
        s1 = split(r1)
        yield
        r2 = dot3(s1, s1)
        yield
        r3 = dot3(split(r2), s1)
        coef = lambda i: by_channel([sums[k][TERMS - 2 - i] for k in range(per)])
        yield
        tail = jnp.where(on_diag, coef(3), 0.0) + coef(4) * r1 + coef(5) * r2 + coef(6) * r3
        poly = (jnp.where(on_diag, coef(0), 0.0) + coef(1) * r1 + coef(2) * r2) + dot3(split(r3), split(tail))
        yield
        vt = dot3(split(poly), split(pt))
        yield
        product = pt * vt
        back = dot3(split(x[:LANES]), split(vt))
        for k in range(per):
            at = k * span
            energy = 0.0
            for j in range(nj):
                low = j * LANES + at
                energy += jnp.sum(product[low : low + span], axis=0, keepdims=True)
            whole = sums[k][TERMS - 1]
            response = antennas * whole - energy * inverse[k]
            factor = lax.rsqrt(response) * lax.rsqrt(bounds[k] * (1.0 / (nj * t_loc)))
            beam = (whole * pt[at : at + span] - back[at : at + span]) * factor
            beam = beam.astype(BF16)
            out_ref[0, g * per + k] = beam[:t_loc]
            out_ref[1, g * per + k] = beam[t_loc:]

    for _ in itertools.zip_longest(*[group_steps(g) for g in range(groups)]):
        pass

    sized(send_ref.at[: antennas - nl], 0).wait_send()
    sized(send_ref, 1).wait_send()


def fused_local(ni, nj, samples, steer_index):
    _, nl, t_loc, _ = samples.shape
    beams, antennas = steer_index.shape
    size = 2 * CH_DEV * t_loc
    vmem = pl.BlockSpec(memory_space=pltpu.VMEM)
    table = jnp.asarray(taper_table(CH_DEV * ni))
    out = pl.pallas_call(
        functools.partial(fused, ni, nj),
        out_shape=pltpu.VMEM((2, CH_DEV, t_loc, beams), BF16),
        in_specs=[pl.BlockSpec(memory_space=pl.ANY)] * 3,
        out_specs=vmem,
        scratch_shapes=[
            pltpu.VMEM((2, nl * t_loc, C), BF16),
            pltpu.VMEM(table.shape, BF16),
            pltpu.VMEM((beams, antennas), jnp.int32),
            pltpu.VMEM((nl * t_loc, CH_DEV * ni), F32),
            pltpu.VMEM((nl * t_loc, CH_DEV * ni), F32),
            pltpu.VMEM((antennas, size), BF16),
            pltpu.VMEM((nj, antennas, size), BF16),
            pltpu.VMEM((4, beams, antennas), BF16),
            pltpu.SemaphoreType.DMA((4,)),
            pltpu.SemaphoreType.DMA,
            pltpu.SemaphoreType.DMA((nj,)),
        ],
        compiler_params=pltpu.CompilerParams(collective_id=0, has_side_effects=True),
    )(samples.reshape(2, nl * t_loc, C), table, steer_index)
    return jnp.transpose(out, (0, 1, 3, 2))


def choose(ni, nj, samples, steer_index):
    _, nl, t_loc, _ = samples.shape
    beams, antennas = steer_index.shape
    tiled = nl == 16 and t_loc == 16 and CH_DEV * ni == LANES and antennas == nl * ni
    if tiled and nj == 2:
        return fused_local(ni, nj, samples, steer_index)
    return local(samples, steer_index)


def solution(mesh):
    return jax.shard_map(
        functools.partial(choose, mesh.shape["chan"], mesh.shape["tm"]),
        mesh=mesh,
        in_specs=(P(None, "chan", "tm", None), P()),
        out_specs=P(None, "chan", None, "tm"),
        check_vma=False,
    )
```
